32 devices in a mesh: grp: 16 (over z, x, core), slab: 2 (over y).
Axes of the slice: x: 2, y: 2, z: 4, core: 2. Of those that a mesh axis runs over, the one named last changes fastest.
Arguments:
- ligand_grids: float32 [2, 4, 128, 128, 128], P(None, None, 'grp', 'slab'), may hold values from -6 to 6
- receptor_kernel: bfloat16 [16, 2, 2, 128, 128, 128], P('grp', None, None, 'slab'), may hold values from -3 to 3
Outputs:
- best_score: bfloat16 [16, 128, 128, 128], P('grp', None, 'slab')
The draws below stay inside these ranges and needn't reach their ends.
All inputs are finite; a program needn't handle non-finite values.
Results may differ from the reference program's by a relative error of at most 0.018.
Values may be sent and summed in bfloat16 or wider, within the bound.
A program may use at most 128 MiB of HBM per device.

```python
import math
import jax
import jax.numpy as jnp
from jax import lax

G = 128
CH = 4
PAIRS = 2
ROT = 2
REC = 16


def block_levels(own_key, dims, split, least, largest):
    factor_of = 1.0
    for position, shards_of in split:
        draws = jax.random.uniform(jax.random.fold_in(jax.random.fold_in(own_key, 6), position), (shards_of,), jnp.float32, least / len(split), largest / len(split))
        factor_of = factor_of * jnp.repeat(jnp.exp(draws), dims[position] // shards_of).reshape((-1,) + (1,) * (len(dims) - 1 - position))
    return factor_of


def scatter_about(key, dims, scale, reach, shards=(), kind=jnp.bfloat16):
    drawn = jax.random.normal(key, dims, jnp.float32) * scale
    if len(shards) > 0:
        drawn = block_levels(key, dims, shards, -0.22, 0.18) * drawn
    return jnp.clip(drawn, min=-reach, max=reach).astype(kind)


def setup_inputs(seed: int = 0) -> dict:
    splits = jax.random.split(jax.random.key(seed), 3)
    ligand_grids = scatter_about(splits[0], (ROT, CH, G, G, G), 1.0, 6.0, ((2, 16), (3, 2)), jnp.float32)
    receptor_kernel = scatter_about(splits[1], (REC, 2, PAIRS, G, G, G), 0.5, 3.0, ((0, 16), (3, 2)))
    return dict(ligand_grids=ligand_grids, receptor_kernel=receptor_kernel)


highest = lax.Precision.HIGHEST

def coefficients(length, inverse):
    positions = jnp.arange(length, dtype=jnp.int32)
    phases = positions[:, None] * positions[None, :] % length
    angles = phases.astype(jnp.float32) * (2.0 * math.pi / length)
    scaling = 1.0 / math.sqrt(length)
    cosine = jnp.cos(angles) * scaling
    sine_part = jnp.sin(angles) * scaling
    if inverse:
        sine_part = -sine_part
    upper_rows = jnp.stack([cosine, sine_part])
    lower_rows = jnp.stack([-sine_part, cosine])
    return jnp.stack([upper_rows, lower_rows])

def pack_pairs(ligand_grids):
    return jnp.stack([ligand_grids[:, 0::2], ligand_grids[:, 1::2]])

def reference(ligand_grids, receptor_kernel):
    length = ligand_grids.shape[4]
    forward = coefficients(length, False)
    forward_low = lax.optimization_barrier(forward.astype(jnp.bfloat16)).astype(jnp.float32)
    inverse_low = lax.optimization_barrier(coefficients(length, True).astype(jnp.bfloat16)).astype(jnp.float32)
    packed = pack_pairs(ligand_grids)
    along_z = jnp.einsum('pqkn,qrjnxy->prjkxy', forward, packed, precision=highest)
    partial_value = jnp.einsum('pqkn,qrjzxn->prjzxk', forward, along_z, precision=highest).astype(jnp.bfloat16)
    spectrum = jnp.einsum('pqkn,qrjznm->prjzkm', forward_low, partial_value.astype(jnp.float32), precision=highest).astype(jnp.bfloat16)
    spec_wide = spectrum.astype(jnp.float32)

    def one_receptor(kernel_one):
        kernel_wide = kernel_one.astype(jnp.float32)
        real_part = lax.optimization_barrier(jnp.sum(kernel_wide[0][None] * spec_wide[0] - kernel_wide[1][None] * spec_wide[1], axis=1))
        imag_part = lax.optimization_barrier(jnp.sum(kernel_wide[0][None] * spec_wide[1] + kernel_wide[1][None] * spec_wide[0], axis=1))
        product = jnp.stack([real_part, imag_part]).astype(jnp.bfloat16).astype(jnp.float32)
        rows_done = jnp.einsum('pqkn,qrznm->przkm', inverse_low, product, precision=highest).astype(jnp.bfloat16).astype(jnp.float32)
        planes = jnp.einsum('pqkn,qrzxn->przxk', inverse_low, rows_done, precision=highest).astype(jnp.bfloat16).astype(jnp.float32)
        scores = jnp.einsum('qkn,qrnxy->rkxy', inverse_low[0], planes, precision=highest)
        return lax.optimization_barrier(jnp.max(scores, axis=0)).astype(jnp.bfloat16)
    return lax.map(one_receptor, receptor_kernel)
```

```python
import math

import functools

import jax
import jax.numpy as jnp
import numpy as np
from jax import lax
from jax.experimental import pallas as pl
from jax.experimental.pallas import tpu as pltpu
from jax.sharding import PartitionSpec as P

highest = lax.Precision.HIGHEST


def coefficients(length, inverse):
    positions = jnp.arange(length, dtype=jnp.int32)
    phases = positions[:, None] * positions[None, :] % length
    angles = phases.astype(jnp.float32) * (2.0 * math.pi / length)
    scaling = 1.0 / math.sqrt(length)
    cosine = jnp.cos(angles) * scaling
    sine_part = jnp.sin(angles) * scaling
    if inverse:
        sine_part = -sine_part
    upper_rows = jnp.stack([cosine, sine_part])
    lower_rows = jnp.stack([-sine_part, cosine])
    return jnp.stack([upper_rows, lower_rows])


def pack_pairs(ligand_piece):
    stacked = jnp.stack([ligand_piece[:, 0::2], ligand_piece[:, 1::2]])
    return stacked.reshape((2, stacked.shape[1] * stacked.shape[2]) + stacked.shape[3:])


def body(ligand_grids, receptor_kernel):
    length = ligand_grids.shape[4]
    rotations = ligand_grids.shape[0]
    channel_pairs = ligand_grids.shape[1] // 2
    forward = coefficients(length, False)
    forward_low = forward.astype(jnp.bfloat16)
    inverse_low = coefficients(length, True).astype(jnp.bfloat16)
    packed = pack_pairs(ligand_grids)
    lines = jnp.einsum("pqkn,qrzxn->pkrzx", forward, packed, precision=highest)
    columns = lax.all_to_all(
        lines.astype(jnp.bfloat16), "grp", split_axis=1, concat_axis=3, tiled=True
    ).astype(lines.dtype)
    partial_value = jnp.einsum("pqkn,qyrnx->pyrkx", forward, columns, precision=highest).astype(
        jnp.bfloat16
    )
    pieces = jnp.einsum(
        "pqkn,qyrzn->pyrzk",
        forward_low,
        lax.all_to_all(partial_value, "slab", split_axis=3, concat_axis=4, tiled=True),
        preferred_element_type=jnp.float32,
    ).astype(jnp.bfloat16)
    collected = lax.all_gather(pieces, "grp", axis=1, tiled=True)
    spectrum = jnp.transpose(collected, (0, 2, 3, 4, 1))
    spec_split = spectrum.reshape((2, rotations, channel_pairs) + spectrum.shape[2:])
    kernel_one = receptor_kernel[0]
    kernel_real = kernel_one[0][None].astype(jnp.float32)
    kernel_imag = kernel_one[1][None].astype(jnp.float32)
    spec_real = spec_split[0].astype(jnp.float32)
    spec_imag = spec_split[1].astype(jnp.float32)
    real_part = jnp.sum(kernel_real * spec_real - kernel_imag * spec_imag, axis=1)
    imag_part = jnp.sum(kernel_real * spec_imag + kernel_imag * spec_real, axis=1)
    product = jnp.stack([real_part, imag_part]).astype(jnp.bfloat16)
    rows_done = jnp.einsum(
        "pqkn,qrznm->przkm", inverse_low, product, preferred_element_type=jnp.float32
    ).astype(jnp.bfloat16)
    planes = jnp.einsum(
        "pqkn,qrzxn->przxk", inverse_low, rows_done, preferred_element_type=jnp.float32
    ).astype(jnp.bfloat16)
    scores = jnp.einsum(
        "qkn,qrnxy->rkxy",
        inverse_low[0],
        lax.all_to_all(planes, "slab", split_axis=3, concat_axis=2, tiled=True),
        preferred_element_type=jnp.float32,
    )
    return jnp.max(scores, axis=0).astype(jnp.bfloat16)[None]


TILE = 16
SUB = 8
f32 = jnp.float32
bf16 = jnp.bfloat16


def waves(length):
    positions = np.arange(length)
    angles = (positions[:, None] * positions[None, :] % length) * (2.0 * math.pi / length)
    scaling = 1.0 / math.sqrt(length)
    cosine, sine = np.cos(angles) * scaling, np.sin(angles) * scaling
    forward = np.stack([np.stack([cosine, sine]), np.stack([-sine, cosine])])
    inverse = np.stack([np.stack([cosine, -sine]), np.stack([sine, cosine])])
    return forward, inverse


def matrices(length, groups):
    forward, inverse = waves(length)
    half, side = length // 2, 2 * length
    block = half // groups
    fz, fx, ix, mz = [], [], [], []
    for own in range(2):
        order = (np.arange(length) + own * half) % length
        by_cell = forward[:, :, order].reshape(2, 2, length, groups, length // groups)
        fz.append(by_cell.transpose(0, 2, 3, 1, 4).reshape(side, side))
        cells = forward[:, :, :, order].reshape(2, 2, length, 2, groups, block)
        fx.append(cells.transpose(0, 2, 4, 3, 1, 5).reshape(side, side))
        ix.append(inverse[:, :, order].transpose(0, 2, 1, 3).reshape(side, side))
        lines = inverse[0][:, :, order].reshape(2, length, length // SUB, SUB)
        mz.append(lines.transpose(1, 2, 0, 3).reshape(length, side))
    fy = forward.transpose(1, 3, 0, 2).reshape(side, side)
    iy = inverse.transpose(1, 3, 0, 2).reshape(side, side)
    return [np.stack(m).astype(np.float32) for m in (fz, fx, ix, mz)] + [
        fy.astype(np.float32),
        iy.astype(np.float32),
    ]


def dot(a, b):
    return jnp.dot(a, b, preferred_element_type=f32)


def split_kernel(rotations, pairs, depth, width, block, lig_ref, out_ref):
    @pl.loop(0, width)
    def _(x):
        for r in range(rotations):
            for j in range(pairs):
                parts = []
                for q in range(2):
                    first = ((r * pairs + j) * 2 + q) * depth * width
                    parts.append(lig_ref[pl.ds(first + x, depth, stride=width), :])
                out_ref[x // block, x % block, r * pairs + j] = jnp.concatenate(parts, 0).astype(bf16)


def zy_kernel(rotations, groups, block, length, fz_ref, fy_ref, in_ref, mine_ref, other_ref, hold):
    fz = fz_ref[...]
    fy = fy_ref[...]
    grids = 2 * rotations

    @pl.loop(0, block)
    def _(x):
        for r in range(rotations):
            cols = [
                jnp.concatenate([in_ref[g, x, 2 * r + j] for g in range(groups)], 0) for j in range(2)
            ]
            lines = dot(fz, jnp.concatenate(cols, 1)).astype(bf16)
            rows = []
            for j in range(2):
                at = slice(j * length, (j + 1) * length)
                rows.append(jnp.concatenate([lines[:length, at], lines[length:, at]], 1))
            plane = dot(jnp.concatenate(rows, 0), fy)
            for p in range(2):
                start = ((p * block + x) * grids + 2 * r) * length
                hold[pl.ds(start, 2 * length), :] = plane[:, p * length : (p + 1) * length]

    stride = grids * length
    half = length // 2

    @pl.loop(0, half, unroll=2)
    def _(k):
        for i in range(grids):
            mine_ref[k, i] = hold[pl.ds(i * length + k, 2 * block, stride=stride), :].astype(bf16)
            other_ref[k, i] = hold[pl.ds(i * length + half + k, 2 * block, stride=stride), :].astype(
                bf16
            )


def score_kernel(rotations, groups, length, fx_ref, ix_ref, iy_ref, rec_ref, in_ref, mine_ref, other_ref, hold):
    fx = fx_ref[...]
    ix = ix_ref[...]
    iy = iy_ref[...]
    rows = rotations * length

    @pl.loop(0, SUB, unroll=2)
    def _(k):
        kr = [rec_ref[0, j, k].astype(f32) for j in range(2)]
        ki = [rec_ref[1, j, k].astype(f32) for j in range(2)]
        real, imag = [], []
        for r in range(rotations):
            cols = [
                jnp.concatenate([in_ref[g, k, 2 * r + j] for g in range(groups)], 0) for j in range(2)
            ]
            spec = dot(fx, jnp.concatenate(cols, 1))
            sr = [spec[:length, j * length : (j + 1) * length] for j in range(2)]
            si = [spec[length:, j * length : (j + 1) * length] for j in range(2)]
            real.append(kr[0] * sr[0] - ki[0] * si[0] + (kr[1] * sr[1] - ki[1] * si[1]))
            imag.append(kr[0] * si[0] + ki[0] * sr[0] + (kr[1] * si[1] + ki[1] * sr[1]))
        product = jnp.concatenate(
            [jnp.concatenate(real, 1).astype(bf16), jnp.concatenate(imag, 1).astype(bf16)], 0
        )
        done = dot(ix, product).astype(bf16)
        flat = []
        for r in range(rotations):
            at = slice(r * length, (r + 1) * length)
            flat.append(jnp.concatenate([done[:length, at], done[length:, at]], 1))
        planes = dot(jnp.concatenate(flat, 0), iy)
        for p in range(2):
            hold[p, pl.ds(k * rows, rows), :] = planes[:, p * length : (p + 1) * length]

    half = length // 2

    @pl.loop(0, half, unroll=4)
    def _(x):
        for r in range(rotations):
            for ref, first in ((mine_ref, 0), (other_ref, half)):
                at = pl.ds(r * length + first + x, SUB, stride=rows)
                ref[r, x, 0] = jnp.concatenate([hold[0, at, :], hold[1, at, :]], 0).astype(bf16)


def last_kernel(rotations, count, length, wide, mz_ref, *refs):
    ins, out_ref, hold = refs[: 2 * count], refs[-2], refs[-1]
    mz = mz_ref[...]

    @pl.loop(0, wide, unroll=2)
    def _(x):
        cols = []
        for r in range(rotations):
            tiles = []
            for ref in ins:
                tiles += [ref[r, x, t] for t in range(ref.shape[2])]
            cols.append(jnp.concatenate(tiles, 0))
        scores = dot(mz, jnp.concatenate(cols, 1))
        best = scores[:, :length]
        for r in range(1, rotations):
            best = jnp.maximum(best, scores[:, r * length : (r + 1) * length])
        hold[pl.ds(x * length, length), :] = best

    @pl.loop(0, length, unroll=4)
    def _(z):
        out_ref[z] = hold[pl.ds(z, wide, stride=length), :].astype(bf16)


CHUNKS = 4


def quick_body(groups, ligand_grids, receptor_kernel):
    rotations, channels, depth, width, length = ligand_grids.shape
    pairs = channels // 2
    grids = rotations * pairs
    half = length // 2
    block = width // groups
    side = 2 * length
    consts = matrices(length, groups)
    own = lax.axis_index("slab")
    fz, fx, ix, mz = [
        lax.dynamic_index_in_dim(jnp.asarray(m).astype(bf16), own, 0, keepdims=False) for m in consts[:4]
    ]
    fy, iy = [jnp.asarray(m).astype(bf16) for m in consts[4:]]
    whole = pl.BlockSpec(memory_space=pltpu.VMEM)

    blocks = pl.pallas_call(
        functools.partial(split_kernel, rotations, pairs, depth, width, block),
        out_shape=jax.ShapeDtypeStruct((groups, block, grids, 2 * depth, length), bf16),
        in_specs=[whole],
        out_specs=whole,
    )(ligand_grids.reshape(-1, length))
    lines = lax.all_to_all(blocks, "grp", split_axis=0, concat_axis=0, tiled=True)
    shape = jax.ShapeDtypeStruct((half, grids, 2 * block, length), bf16)
    mine, other = pl.pallas_call(
        functools.partial(zy_kernel, rotations, groups, block, length),
        out_shape=[shape, shape],
        in_specs=[whole] * 3,
        out_specs=[whole] * 2,
        scratch_shapes=[pltpu.VMEM((2 * block * grids * length, length), f32)],
    )(fz, fy, lines)
    swap = [(0, 1), (1, 0)]
    came = lax.ppermute(other, "slab", swap)
    joined = jnp.concatenate([mine, came], axis=2)

    rec = receptor_kernel[0]
    chunk = half // CHUNKS
    steps = chunk // SUB
    own_parts, far_parts = [], []
    for c in range(CHUNKS):
        gathered = lax.all_gather(joined[c * chunk : (c + 1) * chunk], "grp", axis=0, tiled=False)
        part = jax.ShapeDtypeStruct((rotations, half, steps, TILE, length), bf16)
        keep, send = pl.pallas_call(
            functools.partial(score_kernel, rotations, groups, length),
            grid=(steps,),
            out_shape=[part, part],
            in_specs=[
                pl.BlockSpec((side, side), lambda t: (0, 0)),
                pl.BlockSpec((side, side), lambda t: (0, 0)),
                pl.BlockSpec((side, side), lambda t: (0, 0)),
                pl.BlockSpec((2, pairs, SUB, length, length), lambda t, c=c: (0, 0, c * steps + t, 0, 0)),
                pl.BlockSpec((groups, SUB, grids, TILE, length), lambda t: (0, t, 0, 0, 0)),
            ],
            out_specs=[pl.BlockSpec((rotations, half, 1, TILE, length), lambda t: (0, 0, t, 0, 0))] * 2,
            scratch_shapes=[pltpu.VMEM((2, SUB * rotations * length, length), f32)],
            cost_estimate=pl.CostEstimate(
                flops=chunk * 4 * 2 * side**3, bytes_accessed=10 * 2**20, transcendentals=0
            ),
        )(fx, ix, iy, rec, gathered)
        own_parts.append(keep)
        far_parts.append(lax.ppermute(send, "slab", swap))

    wide = TILE
    best = pl.pallas_call(
        functools.partial(last_kernel, rotations, CHUNKS, length, wide),
        grid=(half // wide,),
        out_shape=jax.ShapeDtypeStruct((length, half, length), bf16),
        in_specs=[pl.BlockSpec((length, side), lambda t: (0, 0))]
        + [pl.BlockSpec((rotations, wide, steps, TILE, length), lambda t: (0, t, 0, 0, 0))] * (2 * CHUNKS),
        out_specs=pl.BlockSpec((length, wide, length), lambda t: (0, t, 0)),
        scratch_shapes=[pltpu.VMEM((wide * length, length), f32)],
    )(mz, *own_parts, *far_parts)
    return best[None]


def choose(groups, slabs, ligand_grids, receptor_kernel):
    rotations, channels, depth, width, length = ligand_grids.shape
    fits = (
        slabs == 2
        and channels == 4
        and rotations == 2
        and depth == SUB
        and width % groups == 0
        and 4 * (width // groups) == TILE
        and length % 128 == 0
        and (length // 2) % (CHUNKS * SUB) == 0
    )
    if fits:
        return quick_body(groups, ligand_grids, receptor_kernel)
    return body(ligand_grids, receptor_kernel)


def solution(mesh):
    return jax.shard_map(
        functools.partial(choose, mesh.shape["grp"], mesh.shape["slab"]),
        mesh=mesh,
        in_specs=(P(None, None, "grp", "slab", None), P("grp", None, None, "slab", None, None)),
        out_specs=P("grp", None, "slab", None),
        check_vma=False,
    )
```

```python
import math

import functools

import jax
import jax.numpy as jnp
import numpy as np
from jax import lax
from jax.experimental import pallas as pl
from jax.experimental.pallas import tpu as pltpu
from jax.sharding import PartitionSpec as P

highest = lax.Precision.HIGHEST


def coefficients(length, inverse):
    positions = jnp.arange(length, dtype=jnp.int32)
    phases = positions[:, None] * positions[None, :] % length
    angles = phases.astype(jnp.float32) * (2.0 * math.pi / length)
    scaling = 1.0 / math.sqrt(length)
    cosine = jnp.cos(angles) * scaling
    sine_part = jnp.sin(angles) * scaling
    if inverse:
        sine_part = -sine_part
    upper_rows = jnp.stack([cosine, sine_part])
    lower_rows = jnp.stack([-sine_part, cosine])
    return jnp.stack([upper_rows, lower_rows])


def pack_pairs(ligand_piece):
    stacked = jnp.stack([ligand_piece[:, 0::2], ligand_piece[:, 1::2]])
    return stacked.reshape((2, stacked.shape[1] * stacked.shape[2]) + stacked.shape[3:])


def body(ligand_grids, receptor_kernel):
    length = ligand_grids.shape[4]
    rotations = ligand_grids.shape[0]
    channel_pairs = ligand_grids.shape[1] // 2
    forward = coefficients(length, False)
    forward_low = forward.astype(jnp.bfloat16)
    inverse_low = coefficients(length, True).astype(jnp.bfloat16)
    packed = pack_pairs(ligand_grids)
    lines = jnp.einsum("pqkn,qrzxn->pkrzx", forward, packed, precision=highest)
    columns = lax.all_to_all(
        lines.astype(jnp.bfloat16), "grp", split_axis=1, concat_axis=3, tiled=True
    ).astype(lines.dtype)
    partial_value = jnp.einsum("pqkn,qyrnx->pyrkx", forward, columns, precision=highest).astype(
        jnp.bfloat16
    )
    pieces = jnp.einsum(
        "pqkn,qyrzn->pyrzk",
        forward_low,
        lax.all_to_all(partial_value, "slab", split_axis=3, concat_axis=4, tiled=True),
        preferred_element_type=jnp.float32,
    ).astype(jnp.bfloat16)
    collected = lax.all_gather(pieces, "grp", axis=1, tiled=True)
    spectrum = jnp.transpose(collected, (0, 2, 3, 4, 1))
    spec_split = spectrum.reshape((2, rotations, channel_pairs) + spectrum.shape[2:])
    kernel_one = receptor_kernel[0]
    kernel_real = kernel_one[0][None].astype(jnp.float32)
    kernel_imag = kernel_one[1][None].astype(jnp.float32)
    spec_real = spec_split[0].astype(jnp.float32)
    spec_imag = spec_split[1].astype(jnp.float32)
    real_part = jnp.sum(kernel_real * spec_real - kernel_imag * spec_imag, axis=1)
    imag_part = jnp.sum(kernel_real * spec_imag + kernel_imag * spec_real, axis=1)
    product = jnp.stack([real_part, imag_part]).astype(jnp.bfloat16)
    rows_done = jnp.einsum(
        "pqkn,qrznm->przkm", inverse_low, product, preferred_element_type=jnp.float32
    ).astype(jnp.bfloat16)
    planes = jnp.einsum(
        "pqkn,qrzxn->przxk", inverse_low, rows_done, preferred_element_type=jnp.float32
    ).astype(jnp.bfloat16)
    scores = jnp.einsum(
        "qkn,qrnxy->rkxy",
        inverse_low[0],
        lax.all_to_all(planes, "slab", split_axis=3, concat_axis=2, tiled=True),
        preferred_element_type=jnp.float32,
    )
    return jnp.max(scores, axis=0).astype(jnp.bfloat16)[None]


TILE = 16
SUB = 8
f32 = jnp.float32
bf16 = jnp.bfloat16


def waves(length):
    positions = np.arange(length)
    angles = (positions[:, None] * positions[None, :] % length) * (2.0 * math.pi / length)
    scaling = 1.0 / math.sqrt(length)
    cosine, sine = np.cos(angles) * scaling, np.sin(angles) * scaling
    forward = np.stack([np.stack([cosine, sine]), np.stack([-sine, cosine])])
    inverse = np.stack([np.stack([cosine, -sine]), np.stack([sine, cosine])])
    return forward, inverse


def matrices(length, groups):
    forward, inverse = waves(length)
    half, side = length // 2, 2 * length
    block = half // groups
    fz, fx, ix, mz = [], [], [], []
    for own in range(2):
        order = (np.arange(length) + own * half) % length
        by_cell = forward[:, :, order].reshape(2, 2, length, groups, length // groups)
        fz.append(by_cell.transpose(0, 2, 3, 1, 4).reshape(side, side))
        cells = forward[:, :, :, order].reshape(2, 2, length, 2, groups, block)
        fx.append(cells.transpose(0, 2, 4, 3, 1, 5).reshape(side, side))
        ix.append(inverse[:, :, order].transpose(0, 2, 1, 3).reshape(side, side))
        lines = inverse[0][:, :, order].reshape(2, length, length // SUB, SUB)
        mz.append(lines.transpose(1, 2, 0, 3).reshape(length, side))
    fy = forward.transpose(1, 3, 0, 2).reshape(side, side)
    iy = inverse.transpose(1, 3, 0, 2).reshape(side, side)
    return [np.stack(m).astype(np.float32) for m in (fz, fx, ix, mz)] + [
        fy.astype(np.float32),
        iy.astype(np.float32),
    ]


def dot(a, b):
    return jnp.dot(a, b, preferred_element_type=f32)


def split_kernel(rotations, pairs, depth, width, block, lig_ref, out_ref):
    @pl.loop(0, width)
    def _(x):
        for r in range(rotations):
            for j in range(pairs):
                parts = []
                for q in range(2):
                    first = ((r * pairs + j) * 2 + q) * depth * width
                    parts.append(lig_ref[pl.ds(first + x, depth, stride=width), :])
                out_ref[x // block, x % block, r * pairs + j] = jnp.concatenate(parts, 0).astype(bf16)


def zy_kernel(rotations, groups, block, length, fz_ref, fy_ref, in_ref, mine_ref, other_ref, hold):
    fz = fz_ref[...]
    fy = fy_ref[...]
    grids = 2 * rotations

    @pl.loop(0, block)
    def _(x):
        for r in range(rotations):
            cols = [
                jnp.concatenate([in_ref[g, x, 2 * r + j] for g in range(groups)], 0) for j in range(2)
            ]
            lines = dot(fz, jnp.concatenate(cols, 1)).astype(bf16)
            rows = []
            for j in range(2):
                at = slice(j * length, (j + 1) * length)
                rows.append(jnp.concatenate([lines[:length, at], lines[length:, at]], 1))
            plane = dot(jnp.concatenate(rows, 0), fy)
            for p in range(2):
                start = ((p * block + x) * grids + 2 * r) * length
                hold[pl.ds(start, 2 * length), :] = plane[:, p * length : (p + 1) * length]

    stride = grids * length
    half = length // 2

    @pl.loop(0, half, unroll=2)
    def _(k):
        for i in range(grids):
            mine_ref[k, i] = hold[pl.ds(i * length + k, 2 * block, stride=stride), :].astype(bf16)
            other_ref[k, i] = hold[pl.ds(i * length + half + k, 2 * block, stride=stride), :].astype(
                bf16
            )


def score_kernel(
    rotations, groups, length, chunks, fx_ref, ix_ref, iy_ref, rec_ref, in_ref, mine_ref, far_ref,
    held, rec, send, hold, rec_sem, own_sem, ring_out, ring_in, pair_out, pair_in, slab_out, slab_in,
):
    me = lax.axis_index("grp")
    slab = lax.axis_index("slab")
    core = lax.rem(me, 2)
    height = groups // 4
    around = groups // 2
    row = me // 4
    column = lax.rem(me // 2, 2)
    spot = jnp.where(column == 0, row, around - 1 - row)

    def device(at, which):
        at = lax.rem(at + around, around)
        return jnp.where(at < height, at * 4, (around - 1 - at) * 4 + 2) + which

    beside = (device(spot + 1, core), device(spot - 1, core))
    partner = device(spot, 1 - core)

    def place(to):
        return {"grp": to, "slab": slab}

    across = {"grp": me, "slab": 1 - slab}
    MESH = pl.DeviceIdType.MESH
    load = pltpu.make_async_copy(rec_ref, rec, rec_sem)
    load.start()
    own = pltpu.make_async_copy(in_ref, held.at[me], own_sem)
    own.start()
    barrier = pltpu.get_barrier_semaphore()
    for to in (place(beside[0]), place(beside[1]), place(partner), across):
        pl.semaphore_signal(barrier, inc=1, device_id=to, device_id_type=MESH)
    pl.semaphore_wait(barrier, 4)
    own.wait()

    def origin(d, t):
        return spot - t if d == 0 else spot + t

    def part(slot, c):
        return held.at[slot, pl.ds(c * SUB, SUB)]

    def ring(d, c, t, slot):
        return pltpu.make_async_remote_copy(
            src_ref=part(slot, c), dst_ref=part(slot, c),
            send_sem=ring_out.at[d, c, t], recv_sem=ring_in.at[d, c, t],
            device_id=place(beside[d]), device_id_type=MESH,
        )

    def ring_send(d, c, t):
        ring(d, c, t, device(origin(d, t), core)).start()

    def ring_wait(d, c, t):
        ring(d, c, t, device(origin(d, t + 1), core)).wait_recv()

    def pair(d, c, t, which):
        slot = device(origin(d, t), which)
        return pltpu.make_async_remote_copy(
            src_ref=part(slot, c), dst_ref=part(slot, c),
            send_sem=pair_out.at[d, c, t], recv_sem=pair_in.at[d, c, t],
            device_id=place(partner), device_id_type=MESH,
        )

    def slab_copy(c):
        return pltpu.make_async_remote_copy(
            src_ref=send.at[c], dst_ref=far_ref.at[c],
            send_sem=slab_out.at[c], recv_sem=slab_in.at[c],
            device_id=across, device_id_type=MESH,
        )

    far_step = around // 2 - 1

    def for_far(c, act):
        for d in range(2):
            @pl.when(lax.rem(c, 2) == d)
            def _():
                act(d)

    def arrived(c, t):
        for d in range(2):
            ring_wait(d, c, t)
            if t + 1 < far_step:
                ring_send(d, c, t + 1)
            pair(d, c, t + 1, core).start()

    rows = rotations * length
    half = length // 2

    def compute(c, first):
        @pl.loop(first, first + SUB // 2, unroll=2)
        def _(k):
            z = c * SUB + k
            kr = [rec[0, j, z].astype(f32) for j in range(2)]
            ki = [rec[1, j, z].astype(f32) for j in range(2)]
            real, imag = [], []
            for r in range(rotations):
                cols = [
                    jnp.concatenate([held[g, z, 2 * r + j] for g in range(groups)], 0)
                    for j in range(2)
                ]
                spec = dot(fx_ref[...], jnp.concatenate(cols, 1))
                sr = [spec[:length, j * length : (j + 1) * length] for j in range(2)]
                si = [spec[length:, j * length : (j + 1) * length] for j in range(2)]
                real.append(kr[0] * sr[0] - ki[0] * si[0] + (kr[1] * sr[1] - ki[1] * si[1]))
                imag.append(kr[0] * si[0] + ki[0] * sr[0] + (kr[1] * si[1] + ki[1] * sr[1]))
            product = jnp.concatenate(
                [jnp.concatenate(real, 1).astype(bf16), jnp.concatenate(imag, 1).astype(bf16)], 0
            )
            done = dot(ix_ref[...], product).astype(bf16)
            flat = []
            for r in range(rotations):
                at = slice(r * length, (r + 1) * length)
                flat.append(jnp.concatenate([done[:length, at], done[length:, at]], 1))
            planes = dot(jnp.concatenate(flat, 0), iy_ref[...])
            for p in range(2):
                hold[p, pl.ds(k * rows, rows), :] = planes[:, p * length : (p + 1) * length]

    def collect(c, ref, first):
        @pl.loop(0, half, unroll=4)
        def _(x):
            for r in range(rotations):
                at = pl.ds(r * length + first + x, SUB, stride=rows)
                ref[c, r, x] = jnp.concatenate([hold[0, at, :], hold[1, at, :]], 0).astype(bf16)

    @pl.loop(0, chunks + 3)
    def _(i):
        c1, c2, c3 = i - 1, i - 2, i - 3

        @pl.when(i < chunks)
        def _():
            for d in range(2):
                ring_send(d, i, 0)
            pair(0, i, 0, core).start()

        @pl.when((c1 >= 0) & (c1 < chunks))
        def _():
            arrived(c1, 1)

        @pl.when((c2 >= 0) & (c2 < chunks))
        def _():
            def act(d):
                ring_wait(d, c2, far_step)
                pair(d, c2, far_step + 1, core).start()

            for_far(c2, act)

        @pl.when(i == 2)
        def _():
            load.wait()

        @pl.when(c3 >= 0)
        def _():
            compute(c3, SUB // 2)
            collect(c3, send, half)
            collect(c3, mine_ref, 0)
            slab_copy(c3).start()

        @pl.when(i < chunks)
        def _():
            arrived(i, 0)

        @pl.when((c1 >= 0) & (c1 < chunks))
        def _():
            arrived(c1, 2)
            for_far(c1, lambda d: ring_send(d, c1, far_step))

        @pl.when((c2 >= 0) & (c2 < chunks))
        def _():
            pair(0, c2, 0, 1 - core).wait_recv()
            for t in range(1, far_step + 1):
                for d in range(2):
                    pair(d, c2, t, 1 - core).wait_recv()
            for_far(c2, lambda d: pair(d, c2, far_step + 1, 1 - core).wait_recv())
            compute(c2, 0)

    @pl.loop(0, chunks)
    def _(c):
        for t in range(far_step):
            for d in range(2):
                ring(d, c, t, device(origin(d, t), core)).wait_send()
                pair(d, c, t + 1, core).wait_send()
        pair(0, c, 0, core).wait_send()

        def act(d):
            ring(d, c, far_step, device(origin(d, far_step), core)).wait_send()
            pair(d, c, far_step + 1, core).wait_send()

        for_far(c, act)
        slab_copy(c).wait_send()
        slab_copy(c).wait_recv()


def last_kernel(rotations, length, wide, mz_ref, mine_ref, far_ref, out_ref, hold):
    mz = mz_ref[...]

    @pl.loop(0, wide, unroll=2)
    def _(x):
        cols = []
        for r in range(rotations):
            tiles = []
            for ref in (mine_ref, far_ref):
                tiles += [ref[t, r, x] for t in range(ref.shape[0])]
            cols.append(jnp.concatenate(tiles, 0))
        scores = dot(mz, jnp.concatenate(cols, 1))
        best = scores[:, :length]
        for r in range(1, rotations):
            best = jnp.maximum(best, scores[:, r * length : (r + 1) * length])
        hold[pl.ds(x * length, length), :] = best

    @pl.loop(0, length, unroll=4)
    def _(z):
        out_ref[z] = hold[pl.ds(z, wide, stride=length), :].astype(bf16)


def quick_body(groups, ligand_grids, receptor_kernel):
    rotations, channels, depth, width, length = ligand_grids.shape
    pairs = channels // 2
    grids = rotations * pairs
    half = length // 2
    block = width // groups
    side = 2 * length
    consts = matrices(length, groups)
    own = lax.axis_index("slab")
    fz, fx, ix, mz = [
        lax.dynamic_index_in_dim(jnp.asarray(m).astype(bf16), own, 0, keepdims=False) for m in consts[:4]
    ]
    fy, iy = [jnp.asarray(m).astype(bf16) for m in consts[4:]]
    whole = pl.BlockSpec(memory_space=pltpu.VMEM)

    blocks = pl.pallas_call(
        functools.partial(split_kernel, rotations, pairs, depth, width, block),
        out_shape=jax.ShapeDtypeStruct((groups, block, grids, 2 * depth, length), bf16),
        in_specs=[whole],
        out_specs=whole,
    )(ligand_grids.reshape(-1, length))
    lines = lax.all_to_all(blocks, "grp", split_axis=0, concat_axis=0, tiled=True)
    shape = jax.ShapeDtypeStruct((half, grids, 2 * block, length), bf16)
    mine, other = pl.pallas_call(
        functools.partial(zy_kernel, rotations, groups, block, length),
        out_shape=[shape, shape],
        in_specs=[whole] * 3,
        out_specs=[whole] * 2,
        scratch_shapes=[pltpu.VMEM((2 * block * grids * length, length), f32)],
    )(fz, fy, lines)
    swap = [(0, 1), (1, 0)]
    came = lax.ppermute(other, "slab", swap)
    joined = jnp.concatenate([mine, came], axis=2)

    rec = receptor_kernel[0]
    chunks = half // SUB
    hops = groups // 4
    part = jax.ShapeDtypeStruct((chunks, rotations, half, TILE, length), bf16)
    dma = pltpu.SemaphoreType.DMA
    keep, far = pl.pallas_call(
        functools.partial(score_kernel, rotations, groups, length, chunks),
        out_shape=[part, part],
        in_specs=[whole] * 3 + [pl.BlockSpec(memory_space=pl.ANY), whole],
        out_specs=[whole] * 2,
        scratch_shapes=[
            pltpu.VMEM((groups,) + joined.shape, bf16),
            pltpu.VMEM(rec.shape, bf16),
            pltpu.VMEM(part.shape, bf16),
            pltpu.VMEM((2, SUB * rotations * length, length), f32),
            dma,
            dma,
            dma((2, chunks, hops)),
            dma((2, chunks, hops)),
            dma((2, chunks, hops + 1)),
            dma((2, chunks, hops + 1)),
            dma((chunks,)),
            dma((chunks,)),
        ],
        compiler_params=pltpu.CompilerParams(
            collective_id=0, has_side_effects=True, vmem_limit_bytes=60 * 2**20
        ),
    )(fx, ix, iy, rec, joined)

    wide = TILE
    best = pl.pallas_call(
        functools.partial(last_kernel, rotations, length, wide),
        grid=(half // wide,),
        out_shape=jax.ShapeDtypeStruct((length, half, length), bf16),
        in_specs=[pl.BlockSpec((length, side), lambda t: (0, 0))]
        + [pl.BlockSpec((chunks, rotations, wide, TILE, length), lambda t: (0, 0, t, 0, 0))] * 2,
        out_specs=pl.BlockSpec((length, wide, length), lambda t: (0, t, 0)),
        scratch_shapes=[pltpu.VMEM((wide * length, length), f32)],
    )(mz, keep, far)
    return best[None]


def choose(groups, slabs, ligand_grids, receptor_kernel):
    rotations, channels, depth, width, length = ligand_grids.shape
    fits = (
        slabs == 2
        and channels == 4
        and rotations == 2
        and depth == SUB
        and width % groups == 0
        and 4 * (width // groups) == TILE
        and length % 128 == 0
        and (length // 2) % SUB == 0
        and groups == 4 * 4
    )
    if fits:
        return quick_body(groups, ligand_grids, receptor_kernel)
    return body(ligand_grids, receptor_kernel)


def solution(mesh):
    return jax.shard_map(
        functools.partial(choose, mesh.shape["grp"], mesh.shape["slab"]),
        mesh=mesh,
        in_specs=(P(None, None, "grp", "slab", None), P("grp", None, None, "slab", None, None)),
        out_specs=P("grp", None, "slab", None),
        check_vma=False,
    )
```

```python
import math

import functools

import jax
import jax.numpy as jnp
import numpy as np
from jax import lax
from jax.experimental import pallas as pl
from jax.experimental.pallas import tpu as pltpu
from jax.sharding import PartitionSpec as P

highest = lax.Precision.HIGHEST


def coefficients(length, inverse):
    positions = jnp.arange(length, dtype=jnp.int32)
    phases = positions[:, None] * positions[None, :] % length
    angles = phases.astype(jnp.float32) * (2.0 * math.pi / length)
    scaling = 1.0 / math.sqrt(length)
    cosine = jnp.cos(angles) * scaling
    sine_part = jnp.sin(angles) * scaling
    if inverse:
        sine_part = -sine_part
    upper_rows = jnp.stack([cosine, sine_part])
    lower_rows = jnp.stack([-sine_part, cosine])
    return jnp.stack([upper_rows, lower_rows])


def pack_pairs(ligand_piece):
    stacked = jnp.stack([ligand_piece[:, 0::2], ligand_piece[:, 1::2]])
    return stacked.reshape((2, stacked.shape[1] * stacked.shape[2]) + stacked.shape[3:])


def body(ligand_grids, receptor_kernel):
    length = ligand_grids.shape[4]
    rotations = ligand_grids.shape[0]
    channel_pairs = ligand_grids.shape[1] // 2
    forward = coefficients(length, False)
    forward_low = forward.astype(jnp.bfloat16)
    inverse_low = coefficients(length, True).astype(jnp.bfloat16)
    packed = pack_pairs(ligand_grids)
    lines = jnp.einsum("pqkn,qrzxn->pkrzx", forward, packed, precision=highest)
    columns = lax.all_to_all(
        lines.astype(jnp.bfloat16), "grp", split_axis=1, concat_axis=3, tiled=True
    ).astype(lines.dtype)
    partial_value = jnp.einsum("pqkn,qyrnx->pyrkx", forward, columns, precision=highest).astype(
        jnp.bfloat16
    )
    pieces = jnp.einsum(
        "pqkn,qyrzn->pyrzk",
        forward_low,
        lax.all_to_all(partial_value, "slab", split_axis=3, concat_axis=4, tiled=True),
        preferred_element_type=jnp.float32,
    ).astype(jnp.bfloat16)
    collected = lax.all_gather(pieces, "grp", axis=1, tiled=True)
    spectrum = jnp.transpose(collected, (0, 2, 3, 4, 1))
    spec_split = spectrum.reshape((2, rotations, channel_pairs) + spectrum.shape[2:])
    kernel_one = receptor_kernel[0]
    kernel_real = kernel_one[0][None].astype(jnp.float32)
    kernel_imag = kernel_one[1][None].astype(jnp.float32)
    spec_real = spec_split[0].astype(jnp.float32)
    spec_imag = spec_split[1].astype(jnp.float32)
    real_part = jnp.sum(kernel_real * spec_real - kernel_imag * spec_imag, axis=1)
    imag_part = jnp.sum(kernel_real * spec_imag + kernel_imag * spec_real, axis=1)
    product = jnp.stack([real_part, imag_part]).astype(jnp.bfloat16)
    rows_done = jnp.einsum(
        "pqkn,qrznm->przkm", inverse_low, product, preferred_element_type=jnp.float32
    ).astype(jnp.bfloat16)
    planes = jnp.einsum(
        "pqkn,qrzxn->przxk", inverse_low, rows_done, preferred_element_type=jnp.float32
    ).astype(jnp.bfloat16)
    scores = jnp.einsum(
        "qkn,qrnxy->rkxy",
        inverse_low[0],
        lax.all_to_all(planes, "slab", split_axis=3, concat_axis=2, tiled=True),
        preferred_element_type=jnp.float32,
    )
    return jnp.max(scores, axis=0).astype(jnp.bfloat16)[None]


TILE = 16
SUB = 8
f32 = jnp.float32
bf16 = jnp.bfloat16


def waves(length):
    positions = np.arange(length)
    angles = (positions[:, None] * positions[None, :] % length) * (2.0 * math.pi / length)
    scaling = 1.0 / math.sqrt(length)
    cosine, sine = np.cos(angles) * scaling, np.sin(angles) * scaling
    forward = np.stack([np.stack([cosine, sine]), np.stack([-sine, cosine])])
    inverse = np.stack([np.stack([cosine, -sine]), np.stack([sine, cosine])])
    return forward, inverse


def matrices(length, groups):
    forward, inverse = waves(length)
    half, side = length // 2, 2 * length
    block = half // groups
    fz, fx, ix, mz = [], [], [], []
    for own in range(2):
        order = (np.arange(length) + own * half) % length
        by_cell = forward[:, :, order].reshape(2, 2, length, groups, length // groups)
        fz.append(by_cell.transpose(0, 2, 3, 1, 4).reshape(side, side))
        cells = forward[:, :, :, order].reshape(2, 2, length, 2, groups, block)
        fx.append(cells.transpose(0, 2, 4, 3, 1, 5).reshape(side, side))
        ix.append(inverse[:, :, order].transpose(0, 2, 1, 3).reshape(side, side))
        lines = inverse[0][:, :, order].reshape(2, length, length // SUB, SUB)
        mz.append(lines.transpose(1, 2, 0, 3).reshape(length, side))
    fy = forward.transpose(1, 3, 0, 2).reshape(side, side)
    iy = inverse.transpose(1, 3, 0, 2).reshape(side, side)
    return [np.stack(m).astype(np.float32) for m in (fz, fx, ix, mz)] + [
        fy.astype(np.float32),
        iy.astype(np.float32),
    ]


def dot(a, b):
    return jnp.dot(a, b, preferred_element_type=f32)


def split_kernel(rotations, pairs, depth, width, block, lig_ref, out_ref):
    @pl.loop(0, width)
    def _(x):
        for r in range(rotations):
            for j in range(pairs):
                parts = []
                for q in range(2):
                    first = ((r * pairs + j) * 2 + q) * depth * width
                    parts.append(lig_ref[pl.ds(first + x, depth, stride=width), :])
                out_ref[x // block, x % block, r * pairs + j] = jnp.concatenate(parts, 0).astype(bf16)


def zy_kernel(rotations, groups, block, length, fz_ref, fy_ref, in_ref, mine_ref, other_ref, hold):
    fz = fz_ref[...]
    fy = fy_ref[...]
    grids = 2 * rotations

    @pl.loop(0, block)
    def _(x):
        for r in range(rotations):
            cols = [
                jnp.concatenate([in_ref[g, x, 2 * r + j] for g in range(groups)], 0) for j in range(2)
            ]
            lines = dot(fz, jnp.concatenate(cols, 1)).astype(bf16)
            rows = []
            for j in range(2):
                at = slice(j * length, (j + 1) * length)
                rows.append(jnp.concatenate([lines[:length, at], lines[length:, at]], 1))
            plane = dot(jnp.concatenate(rows, 0), fy)
            for p in range(2):
                start = ((p * block + x) * grids + 2 * r) * length
                hold[pl.ds(start, 2 * length), :] = plane[:, p * length : (p + 1) * length]

    stride = grids * length
    half = length // 2

    @pl.loop(0, half, unroll=2)
    def _(k):
        for i in range(grids):
            mine_ref[k, i] = hold[pl.ds(i * length + k, 2 * block, stride=stride), :].astype(bf16)
            other_ref[k, i] = hold[pl.ds(i * length + half + k, 2 * block, stride=stride), :].astype(
                bf16
            )


def score_kernel(
    rotations, groups, length, chunks, fx_ref, ix_ref, iy_ref, rec_ref, near_ref, swap_ref, mine_ref, far_ref,
    held, came, rec, send, hold, rec_sem, swap_out, swap_in, ring_out, ring_in, pair_out, pair_in, slab_out, slab_in,
):
    me = lax.axis_index("grp")
    slab = lax.axis_index("slab")
    core = lax.rem(me, 2)
    height = groups // 4
    around = groups // 2
    row = me // 4
    column = lax.rem(me // 2, 2)
    spot = jnp.where(column == 0, row, around - 1 - row)

    def device(at, which):
        at = lax.rem(at + around, around)
        return jnp.where(at < height, at * 4, (around - 1 - at) * 4 + 2) + which

    beside = (device(spot + 1, core), device(spot - 1, core))
    partner = device(spot, 1 - core)

    def place(to):
        return {"grp": to, "slab": slab}

    across = {"grp": me, "slab": 1 - slab}
    MESH = pl.DeviceIdType.MESH
    load = pltpu.make_async_copy(rec_ref, rec, rec_sem)
    load.start()
    barrier = pltpu.get_barrier_semaphore()
    for to in (place(beside[0]), place(beside[1]), place(partner), across):
        pl.semaphore_signal(barrier, inc=1, device_id=to, device_id_type=MESH)
    pl.semaphore_wait(barrier, 4)

    def swap(c):
        at = pl.ds(c * SUB, SUB)
        return pltpu.make_async_remote_copy(
            src_ref=swap_ref.at[at], dst_ref=came.at[at],
            send_sem=swap_out.at[c], recv_sem=swap_in.at[c],
            device_id=across, device_id_type=MESH,
        )

    @pl.loop(0, chunks)
    def _(c):
        swap(c).start()

    def join(c):
        swap(c).wait_recv()

        @pl.loop(0, SUB)
        def _(k):
            z = c * SUB + k
            for g in range(near_ref.shape[1]):
                both = [near_ref[z, g].astype(f32), came[z, g].astype(f32)]
                held[me, z, g] = jnp.concatenate(both, 0).astype(bf16)

    join(0)

    def origin(d, t):
        return spot - t if d == 0 else spot + t

    def part(slot, c):
        return held.at[slot, pl.ds(c * SUB, SUB)]

    def ring(d, c, t, slot):
        return pltpu.make_async_remote_copy(
            src_ref=part(slot, c), dst_ref=part(slot, c),
            send_sem=ring_out.at[d, c, t], recv_sem=ring_in.at[d, c, t],
            device_id=place(beside[d]), device_id_type=MESH,
        )

    def ring_send(d, c, t):
        ring(d, c, t, device(origin(d, t), core)).start()

    def ring_wait(d, c, t):
        ring(d, c, t, device(origin(d, t + 1), core)).wait_recv()

    def pair(d, c, t, which):
        slot = device(origin(d, t), which)
        return pltpu.make_async_remote_copy(
            src_ref=part(slot, c), dst_ref=part(slot, c),
            send_sem=pair_out.at[d, c, t], recv_sem=pair_in.at[d, c, t],
            device_id=place(partner), device_id_type=MESH,
        )

    def slab_copy(c):
        return pltpu.make_async_remote_copy(
            src_ref=send.at[c], dst_ref=far_ref.at[c],
            send_sem=slab_out.at[c], recv_sem=slab_in.at[c],
            device_id=across, device_id_type=MESH,
        )

    far_step = around // 2 - 1

    def for_far(c, act):
        for d in range(2):
            @pl.when(lax.rem(c, 2) == d)
            def _():
                act(d)

    def arrived(c, t):
        for d in range(2):
            ring_wait(d, c, t)
            if t + 1 < far_step:
                ring_send(d, c, t + 1)
            pair(d, c, t + 1, core).start()

    rows = rotations * length
    half = length // 2

    def compute(c, first):
        @pl.loop(first, first + SUB // 2, unroll=2)
        def _(k):
            z = c * SUB + k
            kr = [rec[0, j, z].astype(f32) for j in range(2)]
            ki = [rec[1, j, z].astype(f32) for j in range(2)]
            real, imag = [], []
            for r in range(rotations):
                cols = [
                    jnp.concatenate([held[g, z, 2 * r + j] for g in range(groups)], 0)
                    for j in range(2)
                ]
                spec = dot(fx_ref[...], jnp.concatenate(cols, 1))
                sr = [spec[:length, j * length : (j + 1) * length] for j in range(2)]
                si = [spec[length:, j * length : (j + 1) * length] for j in range(2)]
                real.append(kr[0] * sr[0] - ki[0] * si[0] + (kr[1] * sr[1] - ki[1] * si[1]))
                imag.append(kr[0] * si[0] + ki[0] * sr[0] + (kr[1] * si[1] + ki[1] * sr[1]))
            product = jnp.concatenate(
                [jnp.concatenate(real, 1).astype(bf16), jnp.concatenate(imag, 1).astype(bf16)], 0
            )
            done = dot(ix_ref[...], product).astype(bf16)
            flat = []
            for r in range(rotations):
                at = slice(r * length, (r + 1) * length)
                flat.append(jnp.concatenate([done[:length, at], done[length:, at]], 1))
            planes = dot(jnp.concatenate(flat, 0), iy_ref[...])
            for p in range(2):
                hold[p, pl.ds(k * rows, rows), :] = planes[:, p * length : (p + 1) * length]

    def collect(c, ref, first):
        @pl.loop(0, half, unroll=4)
        def _(x):
            for r in range(rotations):
                at = pl.ds(r * length + first + x, SUB, stride=rows)
                ref[c, r, x] = jnp.concatenate([hold[0, at, :], hold[1, at, :]], 0).astype(bf16)

    @pl.loop(0, chunks + 2)
    def _(i):
        c1, c2 = i - 1, i - 2

        def open_chunk():
            for d in range(2):
                ring_send(d, i, 0)
            pair(0, i, 0, core).start()

        @pl.when((i < chunks) & (i != 1))
        def _():
            open_chunk()

        @pl.when((c1 >= 0) & (c1 < chunks))
        def _():
            arrived(c1, 1)

        @pl.when(i == 1)
        def _():
            open_chunk()

        @pl.when(i == 2)
        def _():
            load.wait()

        @pl.when(c2 >= 0)
        def _():
            def act(d):
                ring_wait(d, c2, far_step)
                pair(d, c2, far_step + 1, core).start()

            for_far(c2, act)
            pair(0, c2, 0, 1 - core).wait_recv()
            for t in range(1, far_step + 1):
                for d in range(2):
                    pair(d, c2, t, 1 - core).wait_recv()
            for_far(c2, lambda d: pair(d, c2, far_step + 1, 1 - core).wait_recv())
            compute(c2, 0)

        @pl.when(i < chunks)
        def _():
            arrived(i, 0)

        @pl.when((c1 >= 0) & (c1 < chunks))
        def _():
            arrived(c1, 2)
            for_far(c1, lambda d: ring_send(d, c1, far_step))

        @pl.when(i + 1 < chunks)
        def _():
            join(i + 1)

        @pl.when(c2 >= 0)
        def _():
            compute(c2, SUB // 2)
            collect(c2, send, half)
            collect(c2, mine_ref, 0)
            slab_copy(c2).start()

    @pl.loop(0, chunks)
    def _(c):
        for t in range(far_step):
            for d in range(2):
                ring(d, c, t, device(origin(d, t), core)).wait_send()
                pair(d, c, t + 1, core).wait_send()
        pair(0, c, 0, core).wait_send()

        def act(d):
            ring(d, c, far_step, device(origin(d, far_step), core)).wait_send()
            pair(d, c, far_step + 1, core).wait_send()

        for_far(c, act)
        swap(c).wait_send()
        slab_copy(c).wait_send()
        slab_copy(c).wait_recv()


def last_kernel(rotations, length, wide, mz_ref, mine_ref, far_ref, out_ref, hold):
    mz = mz_ref[...]

    @pl.loop(0, wide, unroll=2)
    def _(x):
        cols = []
        for r in range(rotations):
            tiles = []
            for ref in (mine_ref, far_ref):
                tiles += [ref[t, r, x] for t in range(ref.shape[0])]
            cols.append(jnp.concatenate(tiles, 0))
        scores = dot(mz, jnp.concatenate(cols, 1))
        best = scores[:, :length]
        for r in range(1, rotations):
            best = jnp.maximum(best, scores[:, r * length : (r + 1) * length])
        hold[pl.ds(x * length, length), :] = best

    @pl.loop(0, length, unroll=4)
    def _(z):
        out_ref[z] = hold[pl.ds(z, wide, stride=length), :].astype(bf16)


def quick_body(groups, ligand_grids, receptor_kernel):
    rotations, channels, depth, width, length = ligand_grids.shape
    pairs = channels // 2
    grids = rotations * pairs
    half = length // 2
    block = width // groups
    side = 2 * length
    consts = matrices(length, groups)
    own = lax.axis_index("slab")
    fz, fx, ix, mz = [
        lax.dynamic_index_in_dim(jnp.asarray(m).astype(bf16), own, 0, keepdims=False) for m in consts[:4]
    ]
    fy, iy = [jnp.asarray(m).astype(bf16) for m in consts[4:]]
    whole = pl.BlockSpec(memory_space=pltpu.VMEM)

    blocks = pl.pallas_call(
        functools.partial(split_kernel, rotations, pairs, depth, width, block),
        out_shape=jax.ShapeDtypeStruct((groups, block, grids, 2 * depth, length), bf16),
        in_specs=[whole],
        out_specs=whole,
    )(ligand_grids.reshape(-1, length))
    lines = lax.all_to_all(blocks, "grp", split_axis=0, concat_axis=0, tiled=True)
    shape = jax.ShapeDtypeStruct((half, grids, 2 * block, length), bf16)
    mine, other = pl.pallas_call(
        functools.partial(zy_kernel, rotations, groups, block, length),
        out_shape=[shape, shape],
        in_specs=[whole] * 3,
        out_specs=[whole] * 2,
        scratch_shapes=[pltpu.VMEM((2 * block * grids * length, length), f32)],
    )(fz, fy, lines)

    rec = receptor_kernel[0]
    chunks = half // SUB
    hops = groups // 4
    part = jax.ShapeDtypeStruct((chunks, rotations, half, TILE, length), bf16)
    dma = pltpu.SemaphoreType.DMA
    keep, far = pl.pallas_call(
        functools.partial(score_kernel, rotations, groups, length, chunks),
        out_shape=[part, part],
        in_specs=[whole] * 3 + [pl.BlockSpec(memory_space=pl.ANY), whole, whole],
        out_specs=[whole] * 2,
        scratch_shapes=[
            pltpu.VMEM((groups, half, grids, TILE, length), bf16),
            pltpu.VMEM(other.shape, bf16),
            pltpu.VMEM(rec.shape, bf16),
            pltpu.VMEM(part.shape, bf16),
            pltpu.VMEM((2, SUB * rotations * length, length), f32),
            dma,
            dma((chunks,)),
            dma((chunks,)),
            dma((2, chunks, hops)),
            dma((2, chunks, hops)),
            dma((2, chunks, hops + 1)),
            dma((2, chunks, hops + 1)),
            dma((chunks,)),
            dma((chunks,)),
        ],
        compiler_params=pltpu.CompilerParams(
            collective_id=0, has_side_effects=True, vmem_limit_bytes=60 * 2**20
        ),
    )(fx, ix, iy, rec, mine, other)

    wide = TILE
    best = pl.pallas_call(
        functools.partial(last_kernel, rotations, length, wide),
        grid=(half // wide,),
        out_shape=jax.ShapeDtypeStruct((length, half, length), bf16),
        in_specs=[pl.BlockSpec((length, side), lambda t: (0, 0))]
        + [pl.BlockSpec((chunks, rotations, wide, TILE, length), lambda t: (0, 0, t, 0, 0))] * 2,
        out_specs=pl.BlockSpec((length, wide, length), lambda t: (0, t, 0)),
        scratch_shapes=[pltpu.VMEM((wide * length, length), f32)],
    )(mz, keep, far)
    return best[None]


def choose(groups, slabs, ligand_grids, receptor_kernel):
    rotations, channels, depth, width, length = ligand_grids.shape
    fits = (
        slabs == 2
        and channels == 4
        and rotations == 2
        and depth == SUB
        and width % groups == 0
        and 4 * (width // groups) == TILE
        and length % 128 == 0
        and (length // 2) % SUB == 0
        and groups == 4 * 4
    )
    if fits:
        return quick_body(groups, ligand_grids, receptor_kernel)
    return body(ligand_grids, receptor_kernel)


def solution(mesh):
    return jax.shard_map(
        functools.partial(choose, mesh.shape["grp"], mesh.shape["slab"]),
        mesh=mesh,
        in_specs=(P(None, None, "grp", "slab", None), P("grp", None, None, "slab", None, None)),
        out_specs=P("grp", None, "slab", None),
        check_vma=False,
    )
```

```python
import math

import functools

import jax
import jax.numpy as jnp
import numpy as np
from jax import lax
from jax.experimental import pallas as pl
from jax.experimental.pallas import tpu as pltpu
from jax.sharding import PartitionSpec as P

highest = lax.Precision.HIGHEST


def coefficients(length, inverse):
    positions = jnp.arange(length, dtype=jnp.int32)
    phases = positions[:, None] * positions[None, :] % length
    angles = phases.astype(jnp.float32) * (2.0 * math.pi / length)
    scaling = 1.0 / math.sqrt(length)
    cosine = jnp.cos(angles) * scaling
    sine_part = jnp.sin(angles) * scaling
    if inverse:
        sine_part = -sine_part
    upper_rows = jnp.stack([cosine, sine_part])
    lower_rows = jnp.stack([-sine_part, cosine])
    return jnp.stack([upper_rows, lower_rows])


def pack_pairs(ligand_piece):
    stacked = jnp.stack([ligand_piece[:, 0::2], ligand_piece[:, 1::2]])
    return stacked.reshape((2, stacked.shape[1] * stacked.shape[2]) + stacked.shape[3:])


def body(ligand_grids, receptor_kernel):
    length = ligand_grids.shape[4]
    rotations = ligand_grids.shape[0]
    channel_pairs = ligand_grids.shape[1] // 2
    forward = coefficients(length, False)
    forward_low = forward.astype(jnp.bfloat16)
    inverse_low = coefficients(length, True).astype(jnp.bfloat16)
    packed = pack_pairs(ligand_grids)
    lines = jnp.einsum("pqkn,qrzxn->pkrzx", forward, packed, precision=highest)
    columns = lax.all_to_all(
        lines.astype(jnp.bfloat16), "grp", split_axis=1, concat_axis=3, tiled=True
    ).astype(lines.dtype)
    partial_value = jnp.einsum("pqkn,qyrnx->pyrkx", forward, columns, precision=highest).astype(
        jnp.bfloat16
    )
    pieces = jnp.einsum(
        "pqkn,qyrzn->pyrzk",
        forward_low,
        lax.all_to_all(partial_value, "slab", split_axis=3, concat_axis=4, tiled=True),
        preferred_element_type=jnp.float32,
    ).astype(jnp.bfloat16)
    collected = lax.all_gather(pieces, "grp", axis=1, tiled=True)
    spectrum = jnp.transpose(collected, (0, 2, 3, 4, 1))
    spec_split = spectrum.reshape((2, rotations, channel_pairs) + spectrum.shape[2:])
    kernel_one = receptor_kernel[0]
    kernel_real = kernel_one[0][None].astype(jnp.float32)
    kernel_imag = kernel_one[1][None].astype(jnp.float32)
    spec_real = spec_split[0].astype(jnp.float32)
    spec_imag = spec_split[1].astype(jnp.float32)
    real_part = jnp.sum(kernel_real * spec_real - kernel_imag * spec_imag, axis=1)
    imag_part = jnp.sum(kernel_real * spec_imag + kernel_imag * spec_real, axis=1)
    product = jnp.stack([real_part, imag_part]).astype(jnp.bfloat16)
    rows_done = jnp.einsum(
        "pqkn,qrznm->przkm", inverse_low, product, preferred_element_type=jnp.float32
    ).astype(jnp.bfloat16)
    planes = jnp.einsum(
        "pqkn,qrzxn->przxk", inverse_low, rows_done, preferred_element_type=jnp.float32
    ).astype(jnp.bfloat16)
    scores = jnp.einsum(
        "qkn,qrnxy->rkxy",
        inverse_low[0],
        lax.all_to_all(planes, "slab", split_axis=3, concat_axis=2, tiled=True),
        preferred_element_type=jnp.float32,
    )
    return jnp.max(scores, axis=0).astype(jnp.bfloat16)[None]


TILE = 16
SUB = 8
f32 = jnp.float32
bf16 = jnp.bfloat16


def waves(length):
    positions = np.arange(length)
    angles = (positions[:, None] * positions[None, :] % length) * (2.0 * math.pi / length)
    scaling = 1.0 / math.sqrt(length)
    cosine, sine = np.cos(angles) * scaling, np.sin(angles) * scaling
    forward = np.stack([np.stack([cosine, sine]), np.stack([-sine, cosine])])
    inverse = np.stack([np.stack([cosine, -sine]), np.stack([sine, cosine])])
    return forward, inverse


def matrices(length, groups):
    forward, inverse = waves(length)
    half, side = length // 2, 2 * length
    block = half // groups
    fz, fx, ix, mz = [], [], [], []
    for own in range(2):
        order = (np.arange(length) + own * half) % length
        by_cell = forward[:, :, order].reshape(2, 2, length, groups, length // groups)
        fz.append(by_cell.transpose(0, 2, 3, 1, 4).reshape(side, side))
        cells = forward[:, :, :, order].reshape(2, 2, length, 2, groups, block)
        fx.append(cells.transpose(0, 2, 4, 3, 1, 5).reshape(side, side))
        ix.append(inverse[:, :, order].transpose(0, 2, 1, 3).reshape(side, side))
        lines = inverse[0][:, :, order].reshape(2, length, length // SUB, SUB)
        mz.append(lines.transpose(1, 2, 0, 3).reshape(length, side))
    fy = forward.transpose(1, 3, 0, 2).reshape(side, side)
    iy = inverse.transpose(1, 3, 0, 2).reshape(side, side)
    return [np.stack(m).astype(np.float32) for m in (fz, fx, ix, mz)] + [
        fy.astype(np.float32),
        iy.astype(np.float32),
    ]


def dot(a, b):
    return jnp.dot(a, b, preferred_element_type=f32)


def split_kernel(rotations, pairs, depth, width, block, lig_ref, out_ref):
    @pl.loop(0, width)
    def _(x):
        for r in range(rotations):
            for j in range(pairs):
                parts = []
                for q in range(2):
                    first = ((r * pairs + j) * 2 + q) * depth * width
                    parts.append(lig_ref[pl.ds(first + x, depth, stride=width), :])
                out_ref[x // block, x % block, r * pairs + j] = jnp.concatenate(parts, 0).astype(bf16)


def zy_kernel(rotations, groups, block, length, fz_ref, fy_ref, in_ref, mine_ref, other_ref, hold):
    fz = fz_ref[...]
    fy = fy_ref[...]
    grids = 2 * rotations

    @pl.loop(0, block)
    def _(x):
        for r in range(rotations):
            cols = [
                jnp.concatenate([in_ref[g, x, 2 * r + j] for g in range(groups)], 0) for j in range(2)
            ]
            lines = dot(fz, jnp.concatenate(cols, 1)).astype(bf16)
            rows = []
            for j in range(2):
                at = slice(j * length, (j + 1) * length)
                rows.append(jnp.concatenate([lines[:length, at], lines[length:, at]], 1))
            plane = dot(jnp.concatenate(rows, 0), fy)
            for p in range(2):
                start = ((p * block + x) * grids + 2 * r) * length
                hold[pl.ds(start, 2 * length), :] = plane[:, p * length : (p + 1) * length]

    stride = grids * length
    half = length // 2

    @pl.loop(0, half, unroll=2)
    def _(k):
        for i in range(grids):
            mine_ref[k, i] = hold[pl.ds(i * length + k, 2 * block, stride=stride), :].astype(bf16)
            other_ref[k, i] = hold[pl.ds(i * length + half + k, 2 * block, stride=stride), :].astype(
                bf16
            )


def score_kernel(
    rotations, groups, length, chunks, fx_ref, ix_ref, iy_ref, mz_ref, rec_ref, near_ref, swap_ref, out_ref,
    mine_ref, far_ref, held, came, rec, send, hold, rec_sem, swap_out, swap_in, ring_out, ring_in, pair_out, pair_in, slab_out, slab_in,
):
    me = lax.axis_index("grp")
    slab = lax.axis_index("slab")
    core = lax.rem(me, 2)
    height = groups // 4
    around = groups // 2
    row = me // 4
    column = lax.rem(me // 2, 2)
    spot = jnp.where(column == 0, row, around - 1 - row)

    def device(at, which):
        at = lax.rem(at + around, around)
        return jnp.where(at < height, at * 4, (around - 1 - at) * 4 + 2) + which

    beside = (device(spot + 1, core), device(spot - 1, core))
    partner = device(spot, 1 - core)

    def place(to):
        return {"grp": to, "slab": slab}

    across = {"grp": me, "slab": 1 - slab}
    MESH = pl.DeviceIdType.MESH
    load = pltpu.make_async_copy(rec_ref, rec, rec_sem)
    load.start()
    barrier = pltpu.get_barrier_semaphore()
    for to in (place(beside[0]), place(beside[1]), place(partner), across):
        pl.semaphore_signal(barrier, inc=1, device_id=to, device_id_type=MESH)
    pl.semaphore_wait(barrier, 4)

    def swap(c):
        at = pl.ds(c * SUB, SUB)
        return pltpu.make_async_remote_copy(
            src_ref=swap_ref.at[at], dst_ref=came.at[at],
            send_sem=swap_out.at[c], recv_sem=swap_in.at[c],
            device_id=across, device_id_type=MESH,
        )

    @pl.loop(0, chunks)
    def _(c):
        swap(c).start()

    def join(c):
        swap(c).wait_recv()

        @pl.loop(0, SUB)
        def _(k):
            z = c * SUB + k
            for g in range(near_ref.shape[1]):
                both = [near_ref[z, g].astype(f32), came[z, g].astype(f32)]
                held[me, z, g] = jnp.concatenate(both, 0).astype(bf16)

    def origin(d, t):
        return spot - t if d == 0 else spot + t

    def part(slot, c):
        return held.at[slot, pl.ds(c * SUB, SUB)]

    def ring(d, c, t, slot):
        return pltpu.make_async_remote_copy(
            src_ref=part(slot, c), dst_ref=part(slot, c),
            send_sem=ring_out.at[d, c, t], recv_sem=ring_in.at[d, c, t],
            device_id=place(beside[d]), device_id_type=MESH,
        )

    def ring_send(d, c, t):
        ring(d, c, t, device(origin(d, t), core)).start()

    def ring_wait(d, c, t):
        ring(d, c, t, device(origin(d, t + 1), core)).wait_recv()

    def pair(d, c, t, which):
        slot = device(origin(d, t), which)
        return pltpu.make_async_remote_copy(
            src_ref=part(slot, c), dst_ref=part(slot, c),
            send_sem=pair_out.at[d, c, t], recv_sem=pair_in.at[d, c, t],
            device_id=place(partner), device_id_type=MESH,
        )

    def slab_copy(c, q):
        at = pl.ds(pl.multiple_of(q * TILE, TILE), TILE)
        return pltpu.make_async_remote_copy(
            src_ref=send.at[c, :, at], dst_ref=far_ref.at[c, :, at],
            send_sem=slab_out.at[c, q], recv_sem=slab_in.at[c, q],
            device_id=across, device_id_type=MESH,
        )

    far_step = around // 2 - 1

    def for_far(c, act):
        for d in range(2):
            @pl.when(lax.rem(c, 2) == d)
            def _():
                act(d)

    def arrived(c, t):
        for d in range(2):
            ring_wait(d, c, t)
            if t + 1 < far_step:
                ring_send(d, c, t + 1)
            pair(d, c, t + 1, core).start()

    rows = rotations * length
    half = length // 2

    def compute(c, first):
        @pl.loop(first, first + SUB // 2, unroll=2)
        def _(k):
            z = c * SUB + k
            kr = [rec[0, j, z].astype(f32) for j in range(2)]
            ki = [rec[1, j, z].astype(f32) for j in range(2)]
            real, imag = [], []
            for r in range(rotations):
                cols = [
                    jnp.concatenate([held[g, z, 2 * r + j] for g in range(groups)], 0)
                    for j in range(2)
                ]
                spec = dot(fx_ref[...], jnp.concatenate(cols, 1))
                sr = [spec[:length, j * length : (j + 1) * length] for j in range(2)]
                si = [spec[length:, j * length : (j + 1) * length] for j in range(2)]
                real.append(kr[0] * sr[0] - ki[0] * si[0] + (kr[1] * sr[1] - ki[1] * si[1]))
                imag.append(kr[0] * si[0] + ki[0] * sr[0] + (kr[1] * si[1] + ki[1] * sr[1]))
            product = jnp.concatenate(
                [jnp.concatenate(real, 1).astype(bf16), jnp.concatenate(imag, 1).astype(bf16)], 0
            )
            done = dot(ix_ref[...], product).astype(bf16)
            flat = []
            for r in range(rotations):
                at = slice(r * length, (r + 1) * length)
                flat.append(jnp.concatenate([done[:length, at], done[length:, at]], 1))
            planes = dot(jnp.concatenate(flat, 0), iy_ref[...])
            for p in range(2):
                hold[p, pl.ds(k * rows, rows), :] = planes[:, p * length : (p + 1) * length]

    def collect(c, ref, first):
        @pl.loop(0, half, unroll=4)
        def _(x):
            for r in range(rotations):
                at = pl.ds(r * length + first + x, SUB, stride=rows)
                ref[c, r, x] = jnp.concatenate([hold[0, at, :], hold[1, at, :]], 0).astype(bf16)

    def open_chunk(c):
        for d in range(2):
            ring_send(d, c, 0)
        pair(0, c, 0, core).start()

    join(0)
    open_chunk(0)

    @pl.loop(0, chunks + 2)
    def _(i):
        c1, c2 = i - 1, i - 2

        @pl.when((c1 >= 0) & (c1 < chunks))
        def _():
            arrived(c1, 1)

        @pl.when(i + 1 < chunks)
        def _():
            join(i + 1)

        @pl.when(i == 2)
        def _():
            load.wait()

        @pl.when(c2 >= 0)
        def _():
            def act(d):
                ring_wait(d, c2, far_step)
                pair(d, c2, far_step + 1, core).start()

            for_far(c2, act)
            pair(0, c2, 0, 1 - core).wait_recv()
            for t in range(1, far_step + 1):
                for d in range(2):
                    pair(d, c2, t, 1 - core).wait_recv()
            for_far(c2, lambda d: pair(d, c2, far_step + 1, 1 - core).wait_recv())
            compute(c2, 0)

        @pl.when(i < chunks)
        def _():
            arrived(i, 0)

        @pl.when((c1 >= 0) & (c1 < chunks))
        def _():
            arrived(c1, 2)
            for_far(c1, lambda d: ring_send(d, c1, far_step))

        @pl.when(i + 1 < chunks)
        def _():
            open_chunk(i + 1)

        @pl.when(c2 >= 0)
        def _():
            compute(c2, SUB // 2)
            collect(c2, send, half)
            collect(c2, mine_ref, 0)
            for q in range(half // TILE):
                slab_copy(c2, q).start()

    @pl.loop(0, chunks)
    def _(c):
        for t in range(far_step):
            for d in range(2):
                ring(d, c, t, device(origin(d, t), core)).wait_send()
                pair(d, c, t + 1, core).wait_send()
        pair(0, c, 0, core).wait_send()

        def act(d):
            ring(d, c, far_step, device(origin(d, far_step), core)).wait_send()
            pair(d, c, far_step + 1, core).wait_send()

        for_far(c, act)
        swap(c).wait_send()

    @pl.loop(0, half // TILE)
    def _(q):
        @pl.loop(0, chunks)
        def _(c):
            slab_copy(c, q).wait_send()
            slab_copy(c, q).wait_recv()

        @pl.loop(0, TILE, unroll=2)
        def _(x):
            cols = []
            for r in range(rotations):
                tiles = [
                    ref[t, r, q * TILE + x] for ref in (mine_ref, far_ref) for t in range(chunks)
                ]
                cols.append(jnp.concatenate(tiles, 0))
            scores = dot(mz_ref[...], jnp.concatenate(cols, 1))
            best = scores[:, :length]
            for r in range(1, rotations):
                best = jnp.maximum(best, scores[:, r * length : (r + 1) * length])
            hold[0, pl.ds(x * length, length), :] = best

        @pl.loop(0, length, unroll=4)
        def _(z):
            at = pl.ds(pl.multiple_of(q * TILE, TILE), TILE)
            out_ref[z, at, :] = hold[0, pl.ds(z, TILE, stride=length), :].astype(bf16)


def quick_body(groups, ligand_grids, receptor_kernel):
    rotations, channels, depth, width, length = ligand_grids.shape
    pairs = channels // 2
    grids = rotations * pairs
    half = length // 2
    block = width // groups
    side = 2 * length
    consts = matrices(length, groups)
    own = lax.axis_index("slab")
    fz, fx, ix, mz = [
        lax.dynamic_index_in_dim(jnp.asarray(m).astype(bf16), own, 0, keepdims=False) for m in consts[:4]
    ]
    fy, iy = [jnp.asarray(m).astype(bf16) for m in consts[4:]]
    whole = pl.BlockSpec(memory_space=pltpu.VMEM)

    blocks = pl.pallas_call(
        functools.partial(split_kernel, rotations, pairs, depth, width, block),
        out_shape=jax.ShapeDtypeStruct((groups, block, grids, 2 * depth, length), bf16),
        in_specs=[whole],
        out_specs=whole,
    )(ligand_grids.reshape(-1, length))
    lines = lax.all_to_all(blocks, "grp", split_axis=0, concat_axis=0, tiled=True)
    shape = jax.ShapeDtypeStruct((half, grids, 2 * block, length), bf16)
    mine, other = pl.pallas_call(
        functools.partial(zy_kernel, rotations, groups, block, length),
        out_shape=[shape, shape],
        in_specs=[whole] * 3,
        out_specs=[whole] * 2,
        scratch_shapes=[pltpu.VMEM((2 * block * grids * length, length), f32)],
    )(fz, fy, lines)

    rec = receptor_kernel[0]
    chunks = half // SUB
    hops = groups // 4
    part = jax.ShapeDtypeStruct((chunks, rotations, half, TILE, length), bf16)
    dma = pltpu.SemaphoreType.DMA
    best = pl.pallas_call(
        functools.partial(score_kernel, rotations, groups, length, chunks),
        out_shape=jax.ShapeDtypeStruct((length, half, length), bf16),
        in_specs=[whole] * 4 + [pl.BlockSpec(memory_space=pl.ANY), whole, whole],
        out_specs=whole,
        scratch_shapes=[
            pltpu.VMEM(part.shape, bf16),
            pltpu.VMEM(part.shape, bf16),
            pltpu.VMEM((groups, half, grids, TILE, length), bf16),
            pltpu.VMEM(other.shape, bf16),
            pltpu.VMEM(rec.shape, bf16),
            pltpu.VMEM(part.shape, bf16),
            pltpu.VMEM((2, SUB * rotations * length, length), f32),
            dma,
            dma((chunks,)),
            dma((chunks,)),
            dma((2, chunks, hops)),
            dma((2, chunks, hops)),
            dma((2, chunks, hops + 1)),
            dma((2, chunks, hops + 1)),
            dma((chunks, half // TILE)),
            dma((chunks, half // TILE)),
        ],
        compiler_params=pltpu.CompilerParams(
            collective_id=0, has_side_effects=True, vmem_limit_bytes=60 * 2**20
        ),
    )(fx, ix, iy, mz, rec, mine, other)

    return best[None]


def choose(groups, slabs, ligand_grids, receptor_kernel):
    rotations, channels, depth, width, length = ligand_grids.shape
    fits = (
        slabs == 2
        and channels == 4
        and rotations == 2
        and depth == SUB
        and width % groups == 0
        and 4 * (width // groups) == TILE
        and length % 128 == 0
        and (length // 2) % SUB == 0
        and groups == 4 * 4
        and (length // 2) % TILE == 0
    )
    if fits:
        return quick_body(groups, ligand_grids, receptor_kernel)
    return body(ligand_grids, receptor_kernel)


def solution(mesh):
    return jax.shard_map(
        functools.partial(choose, mesh.shape["grp"], mesh.shape["slab"]),
        mesh=mesh,
        in_specs=(P(None, None, "grp", "slab", None), P("grp", None, None, "slab", None, None)),
        out_specs=P("grp", None, "slab", None),
        check_vma=False,
    )
```
